128 devices in a mesh: tile: 32 (over x, z, y_lo), ell: 4 (over y_hi, core).
Axes of the slice: x: 4, y: 4 (y_hi: 2, y_lo: 2; y = y_hi * 2 + y_lo), z: 4, core: 2. Of those that a mesh axis runs over, the one named last changes fastest.
Arguments:
- spectra: float32 [55, 15360], P(None, ('tile', 'ell')), may hold values from -1 to 2
- kernel: bfloat16 [15360, 1500], P(('tile', 'ell')), may hold values from -0.046875 to 0.046875
- modes: bfloat16 [1500, 128], replicated, may hold values from -0.15625 to 0.15625
- quads: int32 [4096, 4], replicated, may hold values from 0 to 9
Outputs:
- covariance: float32 [128, 4096, 128], P('ell', 'tile')
The draws below stay inside these ranges and needn't reach their ends.
Inputs may be any that keep to these rules, and one draw needn't show every extreme that they name: `quads`: each row (i, j, k, l) asks for the covariance between the pair of bins (i, j) and the pair (k, l).
All inputs are finite; a program needn't handle non-finite values.
Results may differ from the reference program's by a relative error of at most 0.0025.
Values may be sent and summed in bfloat16 or wider, within the bound.
A program may use at most 128 MiB of HBM per device.

```python
import math
import jax
import jax.numpy as jnp
from jax import lax

NB = 10
NP = 55
L = 15360
NTH = 1500
MODES = 128
QUADS = 4096


def touch_ends(drawn, rng, smallest, largest):
    longest = drawn.shape.index(max(drawn.shape))
    spots = []
    for shift in (0, 1):
        where = [jax.random.randint(jax.random.fold_in(rng, axis), (), 0, length) for axis, length in enumerate(drawn.shape)]
        where[longest] = (where[longest] + shift) % drawn.shape[longest]
        spots.append(tuple(where))
    return drawn.at[spots[0]].set(smallest).at[spots[1]].set(largest)


def level_of(stream_key, shape, split, smallest, largest):
    gain, own = 1.0, jax.random.fold_in(stream_key, 6)
    for axis_at, blocks in split:
        heights = jnp.exp(jax.random.uniform(jax.random.fold_in(own, axis_at), (blocks,), jnp.float32, smallest / len(split), largest / len(split)))
        gain = gain * jnp.repeat(heights, shape[axis_at] // blocks).reshape([-1 if axis == axis_at else 1 for axis in range(len(shape))])
    return gain


def normal_values(rng, extent, width, limit, shards=(), kind=jnp.bfloat16):
    factor_of = level_of(rng, extent, shards, -0.22, 0.18) if shards else 1.0
    array = jax.random.normal(rng, extent, jnp.float32) * width * factor_of
    return jnp.minimum(jnp.maximum(array, -limit), limit).astype(kind)


def setup_inputs(seed: int = 0) -> dict:
    seeds = jax.random.split(jax.random.key(seed), 5)
    return {
        "spectra": jnp.clip(-1.0 + 3.0 * jax.random.uniform(seeds[0], (NP, L), jnp.float32) ** level_of(seeds[0], (NP, L), ((1, 128),), -0.2, 0.2), -1.0, 2.0),
        "kernel": normal_values(seeds[1], (L, NTH), L ** -0.5, 0.046875, ((0, 128),)),
        "modes": normal_values(seeds[2], (NTH, MODES), NTH ** -0.5, 0.15625),
        "quads": touch_ends(jax.random.randint(seeds[3], (QUADS, 4), 0, NB), jax.random.fold_in(seeds[3], 1), 0, NB - 1).astype(jnp.int32),
    }


def pair_index(first, second):
    lower = jnp.minimum(first, second)
    upper = jnp.maximum(first, second)
    return (lower * NB - lower * (lower - 1) // 2 + upper - lower).astype(jnp.int32)

def reference(spectra, kernel, modes, quads):
    compressed = jnp.dot(kernel, modes, preferred_element_type=jnp.float32).astype(jnp.bfloat16)
    positions = jnp.arange(L, dtype=jnp.int32)
    weight = (2 * positions + 5).astype(jnp.float32) * (0.5 / math.sqrt(L))
    first_ik = spectra[pair_index(quads[:, 0], quads[:, 2])]
    second_jl = spectra[pair_index(quads[:, 1], quads[:, 3])]
    third_il = spectra[pair_index(quads[:, 0], quads[:, 3])]
    fourth_jk = spectra[pair_index(quads[:, 1], quads[:, 2])]
    products = weight[None, :] * (first_ik * second_jl + third_il * fourth_jk)

    def single(vector):
        scaled = (vector[:, None] * compressed.astype(jnp.float32)).astype(jnp.bfloat16)
        return jnp.dot(compressed.T, scaled, preferred_element_type=jnp.float32)
    result = lax.map(single, products)
    return jnp.transpose(result, (1, 0, 2))
```

```python
import functools
import math

import jax
import jax.numpy as jnp
from jax import lax
from jax.experimental import pallas as pl
from jax.experimental.pallas import tpu as pltpu
from jax.sharding import PartitionSpec as P

NB = 10
L = 15360
ROWS = 128
SROWS = 64
GROUP = 8
BLOCKS = 64
F32 = jnp.float32
BF16 = jnp.bfloat16


def pair_index(first, second):
    lower = jnp.minimum(first, second)
    upper = jnp.maximum(first, second)
    return lower * NB - lower * (lower - 1) // 2 + upper - lower


def contraction(pairs, c_ref, s_ref, mine, theirs, left, right, lhs, wide, prods, acc):
    ell = lax.axis_index("ell")
    half, core = ell // 2, ell % 2
    lane = lax.broadcasted_iota(jnp.int32, (ROWS, 128), 1)
    sublane = lax.broadcasted_iota(jnp.int32, (GROUP, 128), 0)
    lane8 = lax.broadcasted_iota(jnp.int32, (GROUP, 128), 1)
    scale = 0.5 / math.sqrt(L)

    def block(group, j):
        return lax.rem(group * GROUP + j, BLOCKS)

    def weights(group):
        base = jnp.zeros((GROUP, 128), jnp.int32)
        for j in range(GROUP):
            base = jnp.where(sublane == j, (2 * block(group, j) + core) * 120, base)
        return (2 * (base + lane8) + 5).astype(F32) * scale

    def widen(group):
        for j in range(GROUP):
            wide[j * SROWS : (j + 1) * SROWS, :] = s_ref[block(group, j)].astype(F32)

    def product(q, weight):
        ik, jl, il, jk = (
            wide[pl.ds(pairs[k, q], GROUP, stride=SROWS), :] for k in range(4)
        )
        prods[pl.ds(q, GROUP, stride=128), :] = weight * (ik * jl + il * jk)

    def finish(slot):
        for j in range(GROUP):
            lhs[slot, :, j * ROWS : (j + 1) * ROWS] = prods[j * 128 : (j + 1) * 128, :].astype(BF16)

    def pattern(slot, group, j, i):
        x = c_ref[block(group, j)].astype(F32)
        rows = slice(j * ROWS, (j + 1) * ROWS)
        if i < 8:
            at = half * 64 + lax.rem(core * 32 + 8 * i, 64) + lane // 16
            left[slot, i, rows, :] = jnp.take_along_axis(x, at, axis=1).astype(BF16)
        else:
            at = 16 * (i - 8) + lane % 16
            right[slot, i - 8, rows, :] = jnp.take_along_axis(x, at, axis=1).astype(BF16)

    every = [(j, i) for j in range(GROUP) for i in range(16)]

    widen(0)
    first_weight = weights(0)
    lax.fori_loop(0, 128, lambda q, _: product(q, first_weight), None)
    finish(0)
    for j, i in every:
        pattern(0, 0, j, i)
    acc[...] = jnp.zeros_like(acc)

    def two(step, _):
        for slot in range(2):
            following = step * 2 + slot + 1
            widen(following)
            weight = weights(following)
            for n in range(32):
                for j, i in every[4 * n : 4 * n + 4]:
                    pattern(1 - slot, following, j, i)
                for q in range(4 * n, 4 * n + 4):
                    product(q, weight)
                rhs = jnp.concatenate(
                    [left[slot, m // 8] * right[slot, m % 8] for m in (2 * n, 2 * n + 1)], axis=1
                )
                acc[:, n * 256 : (n + 1) * 256] += jnp.dot(
                    lhs[slot], rhs, preferred_element_type=F32
                )
            finish(1 - slot)

    lax.fori_loop(0, BLOCKS // GROUP // 2, two, None)
    mine[...] = acc[:, :4096]
    theirs[...] = acc[:, 4096:].astype(BF16)


def contract(pairs, c_all, s_all):
    vmem = pl.BlockSpec(memory_space=pltpu.VMEM)
    return pl.pallas_call(
        contraction,
        out_shape=(
            jax.ShapeDtypeStruct((128, 4096), F32),
            jax.ShapeDtypeStruct((128, 4096), BF16),
        ),
        in_specs=[pl.BlockSpec(memory_space=pltpu.SMEM), vmem, vmem],
        out_specs=(vmem, vmem),
        scratch_shapes=[
            pltpu.VMEM((2, 8, GROUP * ROWS, 128), BF16),
            pltpu.VMEM((2, 8, GROUP * ROWS, 128), BF16),
            pltpu.VMEM((2, 128, GROUP * ROWS), BF16),
            pltpu.VMEM((GROUP * SROWS, 128), F32),
            pltpu.VMEM((GROUP * 128, 128), F32),
            pltpu.VMEM((128, 8192), F32),
        ],
        compiler_params=pltpu.CompilerParams(vmem_limit_bytes=60 * 2**20),
    )(pairs, c_all, s_all)


def spread(mine, theirs, out):
    lane = lax.broadcasted_iota(jnp.int32, (128, 128), 1)
    cols = [slice(j * 128, (j + 1) * 128) for j in range(8)]
    v = [mine[:, c] + theirs[:, c].astype(F32) for c in cols]
    for k in (1, 2, 4):
        low = (lane // 16) & k == 0
        for m in range(8):
            if m & k == 0:
                a, b = v[m], v[m + k]
                v[m] = jnp.where(low, a, pltpu.roll(b, 16 * k, 1))
                v[m + k] = jnp.where(low, pltpu.roll(a, 128 - 16 * k, 1), b)
    for m in range(8):
        out[m] = v[m]


def combine(mine, theirs):
    return pl.pallas_call(
        spread,
        out_shape=jax.ShapeDtypeStruct((32, 128, 128), F32),
        grid=(4,),
        in_specs=[pl.BlockSpec((128, 1024), lambda i: (0, i))] * 2,
        out_specs=pl.BlockSpec((8, 128, 128), lambda i: (i, 0, 0)),
    )(mine, theirs)


def body(spectra, kernel, modes, quads):
    tile_count, ell_count = lax.axis_size("tile"), lax.axis_size("ell")
    compressed = jnp.dot(kernel, modes, preferred_element_type=F32).astype(BF16)
    local = jnp.concatenate(
        [
            jnp.pad(compressed, ((0, ROWS - 120), (0, 0))),
            jnp.pad(spectra.astype(BF16), ((0, SROWS - 55), (0, ROWS - 120))),
        ]
    )
    groups = [
        [4 * t + 2 * h + core for t in range(tile_count) for h in range(ell_count // 2)]
        for core in range(2)
    ]
    every = lax.all_gather(local, ("tile", "ell"), axis_index_groups=groups)
    own = lax.dynamic_slice_in_dim(quads, lax.axis_index("tile") * 128, 128, 0).T
    i, j, k, l = own[0], own[1], own[2], own[3]
    pairs = jnp.stack([pair_index(i, k), pair_index(j, l), pair_index(i, l), pair_index(j, k)])
    mine, theirs = contract(pairs, every[:, :ROWS], every[:, ROWS:])
    theirs = lax.ppermute(theirs, "ell", [(0, 1), (1, 0), (2, 3), (3, 2)])
    return combine(mine, theirs)


def solution(mesh):
    return jax.shard_map(
        body,
        mesh=mesh,
        in_specs=(P(None, ("tile", "ell")), P(("tile", "ell"), None), P(), P()),
        out_specs=P("ell", "tile", None),
        check_vma=False,
    )
```

```python
import functools
import math

import jax
import jax.numpy as jnp
from jax import lax
from jax.experimental import pallas as pl
from jax.experimental.pallas import tpu as pltpu
from jax.sharding import PartitionSpec as P

NB = 10
L = 15360
ROWS = 128
SROWS = 64
WIDE = 57
TALL = 129
GROUP = 8
BLOCKS = 64
F32 = jnp.float32
BF16 = jnp.bfloat16
MESH = pl.DeviceIdType.MESH
ORDERS = ((0, 1, 2), (1, 2, 0), (2, 0, 1))


def pair_index(first, second):
    lower = jnp.minimum(first, second)
    upper = jnp.maximum(first, second)
    return lower * NB - lower * (lower - 1) // 2 + upper - lower


def place(e):
    group = e[0] // 2 * 4 + e[1] // 2 * 2 + e[2] // 2
    return group, e[0] % 2 * 4 + e[1] % 2 * 2 + e[2] % 2


def fused(
    pairs, local, out, top, low, spec, left, right, lhs, wide, prods, acc, sent, got,
    own_sem, send_sem, recv_sem, swap_send, swap_recv,
):
    tile, ell = lax.axis_index("tile"), lax.axis_index("ell")
    half, core = ell // 2, ell % 2
    chip = (tile // 8, half * 2 + tile % 2, tile // 2 % 4)
    parts = (top, low, spec)

    def device(x, y, z, on):
        return ((x * 4 + z) * 2 + y % 2, y // 2 * 2 + on)

    def peer(axis, k):
        at = list(chip)
        at[axis] = (at[axis] + k) % 4
        return device(*at, core)

    partner = device(*chip, 1 - core)
    barrier = pltpu.get_barrier_semaphore()
    for axis in range(3):
        for k in (1, 2, 3):
            pl.semaphore_signal(barrier, inc=1, device_id=peer(axis, k), device_id_type=MESH)
    pl.semaphore_signal(barrier, inc=1, device_id=partner, device_id_type=MESH)
    pl.semaphore_wait(barrier, 10)

    def send(p, src, dst, axis, k, send_at, recv_at):
        pltpu.make_async_remote_copy(
            src_ref=src,
            dst_ref=parts[p].at[place(dst)],
            send_sem=send_sem.at[p, send_at],
            recv_sem=recv_sem.at[p, recv_at],
            device_id=peer(axis, k),
            device_id_type=MESH,
        ).start()

    def wait(p, ref, sem):
        pltpu.make_async_copy(ref, ref, sem).wait()

    for p, (d1, d2, d3) in enumerate(ORDERS):
        mine = local.at[pl.ds(64 * p, 64)]
        pltpu.make_async_copy(mine, parts[p].at[0, 0], own_sem.at[p]).start()
        for k in (1, 2, 3):
            e = [0, 0, 0]
            e[d1] = k
            send(p, mine, e, d1, k, 0, 0)
    for p, (d1, d2, d3) in enumerate(ORDERS):
        wait(p, parts[p].at[0, 0], own_sem.at[p])
        wait(p, parts[p].at[0, pl.ds(0, 3)], recv_sem.at[p, 0])
        for k in (1, 3, 2):
            for m in range(4):
                e = [0, 0, 0]
                e[d1] = m
                src = parts[p].at[place(e)]
                e[d2] = k
                send(p, src, e, d2, k, 1, 1)
    for p in range(3):
        wait(p, parts[p].at[pl.ds(0, 3), pl.ds(0, 4)], recv_sem.at[p, 1])
    for group in range(8):
        high = (group // 4, group // 2 % 2, group % 2)
        for p, (d1, d2, d3) in enumerate(ORDERS):
            for k in (1, 3, 2):
                if k // 2 != high[d3]:
                    continue
                for m in range(4):
                    e = [0, 0, 0]
                    e[d1] = 2 * high[d1] + m // 2
                    e[d2] = 2 * high[d2] + m % 2
                    src = parts[p].at[place(e)]
                    e[d3] = k
                    send(p, src, e, d3, k, 2, 2 + group)

    def arrive(group):
        high = (group // 4, group // 2 % 2, group % 2)
        for p, (d1, d2, d3) in enumerate(ORDERS):
            sem = recv_sem.at[p, 2 + group]

            @pl.when(high[d3] == 0)
            def _():
                wait(p, parts[p].at[0, pl.ds(0, 4)], sem)

            @pl.when(high[d3] == 1)
            def _():
                wait(p, parts[p].at[0], sem)

    lane = lax.broadcasted_iota(jnp.int32, (64, 128), 1)
    sublane = lax.broadcasted_iota(jnp.int32, (GROUP, 128), 0)
    lane8 = lax.broadcasted_iota(jnp.int32, (GROUP, 128), 1)
    scale = 0.5 / math.sqrt(L)

    def weights(group):
        base = jnp.zeros((GROUP, 128), jnp.int32)
        high = (group // 4, group // 2 % 2, group % 2)
        for j in range(GROUP):
            offset = (j // 4, j // 2 % 2, j % 2)
            x, y, z = ((c + 4 - 2 * h - o) % 4 for c, h, o in zip(chip, high, offset))
            at = ((x * 4 + z) * 2 + y % 2) * 4 + y // 2 * 2 + core
            base = jnp.where(sublane == j, at * 120, base)
        return (2 * (base + lane8) + 5).astype(F32) * scale

    def widen(group):
        for j in range(GROUP):
            wide[j * WIDE : j * WIDE + 56, :] = spec[group, j][:56].astype(F32)

    def product(q, weight):
        ik, jl, il, jk = (wide[pl.ds(pairs[k, q], GROUP, stride=WIDE), :] for k in range(4))
        prods[pl.ds(q, GROUP, stride=TALL), :] = weight * (ik * jl + il * jk)

    def finish(slot):
        for j in range(GROUP):
            rows = prods[j * TALL : j * TALL + 128, :]
            lhs[slot, :, j * ROWS : (j + 1) * ROWS] = rows.astype(BF16)

    def pattern(slot, group, j, i):
        for h, ref in enumerate((top, low)):
            x = ref[group, j].astype(F32)
            rows = slice(j * ROWS + 64 * h, j * ROWS + 64 * h + 64)
            if i < 8:
                at = half * 64 + (core * 32 + 8 * i) % 64 + lane // 16
                left[slot, i, rows, :] = jnp.take_along_axis(x, at, axis=1).astype(BF16)
            else:
                at = 16 * (i - 8) + lane % 16
                right[slot, i - 8, rows, :] = jnp.take_along_axis(x, at, axis=1).astype(BF16)

    every = [(j, i) for j in range(GROUP) for i in range(16)]

    acc[...] = jnp.zeros_like(acc)
    arrive(0)
    widen(0)
    first_weight = weights(0)
    lax.fori_loop(0, 128, lambda q, _: product(q, first_weight), None, unroll=8)
    finish(0)
    for j, i in every:
        pattern(0, 0, j, i)

    def two(step, _):
        for slot in range(2):
            ahead = step * 2 + slot + 1

            @pl.when(ahead < 8)
            def _():
                arrive(ahead)

            following = ahead % 8
            widen(following)
            weight = weights(following)
            for n in range(32):
                for j, i in every[4 * n : 4 * n + 4]:
                    pattern(1 - slot, following, j, i)
                for q in range(4 * n, 4 * n + 4):
                    product(q, weight)
                rhs = jnp.concatenate(
                    [left[slot, m // 8] * right[slot, m % 8] for m in (2 * n, 2 * n + 1)], axis=1
                )
                acc[:, n * 256 : (n + 1) * 256] += jnp.dot(
                    lhs[slot], rhs, preferred_element_type=F32
                )
            finish(1 - slot)

    lax.fori_loop(0, BLOCKS // GROUP // 2, two, None)

    def swap(i):
        return pltpu.make_async_remote_copy(
            src_ref=sent.at[i],
            dst_ref=got.at[i],
            send_sem=swap_send.at[i],
            recv_sem=swap_recv.at[i],
            device_id=partner,
            device_id_type=MESH,
        )

    for i in range(4):
        sent[i] = acc[:, 4096 + i * 1024 : 5120 + i * 1024].astype(BF16)
        swap(i).start()
    for p in range(3):
        wait(p, parts[p].at[0, pl.ds(0, 3)], send_sem.at[p, 0])
        wait(p, parts[p].at[pl.ds(0, 3), pl.ds(0, 4)], send_sem.at[p, 1])
        wait(p, parts[p].at[pl.ds(0, 6)], send_sem.at[p, 2])
    lane = lax.broadcasted_iota(jnp.int32, (128, 128), 1)
    for i in range(4):
        swap(i).wait()
        v = [
            acc[:, i * 1024 + j * 128 : i * 1024 + (j + 1) * 128]
            + got[i, :, j * 128 : (j + 1) * 128].astype(F32)
            for j in range(8)
        ]
        for k in (1, 2, 4):
            under = (lane // 16) & k == 0
            for m in range(8):
                if m & k == 0:
                    a, b = v[m], v[m + k]
                    v[m] = jnp.where(under, a, pltpu.roll(b, 16 * k, 1))
                    v[m + k] = jnp.where(under, pltpu.roll(a, 128 - 16 * k, 1), b)
        for m in range(8):
            out[i * 8 + m] = v[m]


def covariance(pairs, local):
    vmem = pl.BlockSpec(memory_space=pltpu.VMEM)
    return pl.pallas_call(
        fused,
        out_shape=jax.ShapeDtypeStruct((32, 128, 128), F32),
        in_specs=[pl.BlockSpec(memory_space=pltpu.SMEM), vmem],
        out_specs=vmem,
        scratch_shapes=[
            pltpu.VMEM((8, 8, 64, 128), BF16),
            pltpu.VMEM((8, 8, 64, 128), BF16),
            pltpu.VMEM((8, 8, 64, 128), BF16),
            pltpu.VMEM((2, 8, GROUP * ROWS, 128), BF16),
            pltpu.VMEM((2, 8, GROUP * ROWS, 128), BF16),
            pltpu.VMEM((2, 128, GROUP * ROWS), BF16),
            pltpu.VMEM((GROUP * WIDE, 128), F32),
            pltpu.VMEM((GROUP * TALL, 128), F32),
            pltpu.VMEM((128, 8192), F32),
            pltpu.VMEM((4, 128, 1024), BF16),
            pltpu.VMEM((4, 128, 1024), BF16),
            pltpu.SemaphoreType.DMA((3,)),
            pltpu.SemaphoreType.DMA((3, 3)),
            pltpu.SemaphoreType.DMA((3, 10)),
            pltpu.SemaphoreType.DMA((4,)),
            pltpu.SemaphoreType.DMA((4,)),
        ],
        compiler_params=pltpu.CompilerParams(
            collective_id=0, has_side_effects=True, vmem_limit_bytes=60 * 2**20
        ),
    )(pairs, local)


def body(spectra, kernel, modes, quads):
    compressed = jnp.dot(kernel, modes, preferred_element_type=F32).astype(BF16)
    local = jnp.concatenate(
        [
            jnp.pad(compressed, ((0, ROWS - 120), (0, 0))),
            jnp.pad(spectra.astype(BF16), ((0, SROWS - 55), (0, ROWS - 120))),
        ]
    )
    own = lax.dynamic_slice_in_dim(quads, lax.axis_index("tile") * 128, 128, 0).T
    i, j, k, l = own[0], own[1], own[2], own[3]
    pairs = jnp.stack([pair_index(i, k), pair_index(j, l), pair_index(i, l), pair_index(j, k)])
    return covariance(pairs, local)


def solution(mesh):
    return jax.shard_map(
        body,
        mesh=mesh,
        in_specs=(P(None, ("tile", "ell")), P(("tile", "ell"), None), P(), P()),
        out_specs=P("ell", "tile", None),
        check_vma=False,
    )
```

```python
import functools
import math

import jax
import jax.numpy as jnp
from jax import lax
from jax.experimental import pallas as pl
from jax.experimental.pallas import tpu as pltpu
from jax.sharding import PartitionSpec as P

NB = 10
L = 15360
ROWS = 128
SROWS = 64
WIDE = 57
TALL = 129
GROUP = 8
BLOCKS = 64
F32 = jnp.float32
BF16 = jnp.bfloat16
MESH = pl.DeviceIdType.MESH
ORDERS = ((0, 1, 2), (1, 2, 0), (2, 0, 1))


def pair_index(first, second):
    lower = jnp.minimum(first, second)
    upper = jnp.maximum(first, second)
    return lower * NB - lower * (lower - 1) // 2 + upper - lower


def place(e):
    group = e[0] // 2 * 4 + e[1] // 2 * 2 + e[2] // 2
    return group, e[0] % 2 * 4 + e[1] % 2 * 2 + e[2] % 2


def fused(
    pairs, spectra, kernel, modes, out, local, top, low, spec, left, right, lhs, wide, prods, acc,
    sent, got, own_sem, send_sem, recv_sem, swap_send, swap_recv,
):
    tile, ell = lax.axis_index("tile"), lax.axis_index("ell")
    half, core = ell // 2, ell % 2
    chip = (tile // 8, half * 2 + tile % 2, tile // 2 % 4)
    parts = (top, low, spec)

    def device(x, y, z, on):
        return ((x * 4 + z) * 2 + y % 2, y // 2 * 2 + on)

    def peer(axis, k):
        at = list(chip)
        at[axis] = (at[axis] + k) % 4
        return device(*at, core)

    partner = device(*chip, 1 - core)
    barrier = pltpu.get_barrier_semaphore()
    for axis in range(3):
        for k in (1, 2, 3):
            pl.semaphore_signal(barrier, inc=1, device_id=peer(axis, k), device_id_type=MESH)
    pl.semaphore_signal(barrier, inc=1, device_id=partner, device_id_type=MESH)

    compressed = jnp.dot(kernel[...], modes[...], preferred_element_type=F32)
    local[...] = jnp.zeros_like(local)
    local[:120, :] = compressed.astype(BF16)
    local[128:183, :120] = spectra[...].astype(BF16)
    acc[...] = jnp.zeros_like(acc)
    pl.semaphore_wait(barrier, 10)

    def send(p, src, dst, axis, k, send_at, recv_at):
        pltpu.make_async_remote_copy(
            src_ref=src,
            dst_ref=parts[p].at[place(dst)],
            send_sem=send_sem.at[p, send_at],
            recv_sem=recv_sem.at[p, recv_at],
            device_id=peer(axis, k),
            device_id_type=MESH,
        ).start()

    def wait(p, ref, sem):
        pltpu.make_async_copy(ref, ref, sem).wait()

    for p, (d1, d2, d3) in enumerate(ORDERS):
        mine = local.at[pl.ds(64 * p, 64)]
        pltpu.make_async_copy(mine, parts[p].at[0, 0], own_sem.at[p]).start()
        for k in (1, 2, 3):
            e = [0, 0, 0]
            e[d1] = k
            send(p, mine, e, d1, k, 0, 0)
    for p, (d1, d2, d3) in enumerate(ORDERS):
        wait(p, parts[p].at[0, 0], own_sem.at[p])
        wait(p, parts[p].at[0, pl.ds(0, 3)], recv_sem.at[p, 0])
        for step in range(4):
            for k, m in ((1, step), (3, 3 - step)):
                e = [0, 0, 0]
                e[d1] = m
                src = parts[p].at[place(e)]
                e[d2] = k
                on = {(1, True): 1, (3, False): 2}.get((k, m < 2), 3)
                send(p, src, e, d2, k, 1, on)
    for p, (d1, d2, d3) in enumerate(ORDERS):
        for k, lines in ((1, (0, 1)), (3, (2, 3))):
            wait(p, parts[p].at[0, pl.ds(0, 2)], recv_sem.at[p, 1 + k // 2])
            for m in lines:
                e = [0, 0, 0]
                e[d1], e[d2] = m, k
                src = parts[p].at[place(e)]
                e[d2] = 2
                send(p, src, e, d2, k, 1, 3)

    def four(p, quarter, came, k, lands):
        d1, d2, d3 = ORDERS[p]
        for m in range(4):
            e = [0, 0, 0]
            e[d1], e[d2], e[d3] = quarter // 2 * 2 + m // 2, quarter % 2 * 2 + m % 2, came
            src = parts[p].at[place(e)]
            e[d3] = lands
            send(p, src, e, d3, k, 2, 4 + 3 * quarter + lands - 1)

    def landed(p, quarter, k):
        wait(p, parts[p].at[0, pl.ds(0, 4)], recv_sem.at[p, 4 + 3 * quarter + k - 1])

    def forward(p, quarter, k):
        landed(p, quarter, k)
        four(p, quarter, k, k, 2)

    for p in range(3):
        wait(p, parts[p].at[0], recv_sem.at[p, 3])
        for ahead, back in ((0, 1), (3, 2)):
            four(p, ahead, 0, 1, 1)
            four(p, back, 0, 3, 3)
    for p in range(3):
        for ahead, back in ((1, 0), (2, 3)):
            four(p, ahead, 0, 1, 1)
            four(p, back, 0, 3, 3)

    def arrive(group):
        high = (group // 4, group // 2 % 2, group % 2)
        for p, (d1, d2, d3) in enumerate(ORDERS):
            quarter = 2 * high[d1] + high[d2]
            mixed = (high[d1] + high[d2]) % 2

            @pl.when((1 - high[d3]) * mixed == 1)
            def _():
                landed(p, quarter, 1)

            @pl.when(high[d3] == 1)
            def _():
                landed(p, quarter, 2)

            @pl.when(high[d3] * (1 - mixed) == 1)
            def _():
                landed(p, quarter, 3)

    lane = lax.broadcasted_iota(jnp.int32, (64, 128), 1)
    sublane = lax.broadcasted_iota(jnp.int32, (GROUP, 128), 0)
    lane8 = lax.broadcasted_iota(jnp.int32, (GROUP, 128), 1)
    scale = 0.5 / math.sqrt(L)

    def weights(group):
        base = jnp.zeros((GROUP, 128), jnp.int32)
        high = (group // 4, group // 2 % 2, group % 2)
        for j in range(GROUP):
            offset = (j // 4, j // 2 % 2, j % 2)
            x, y, z = ((c + 4 - 2 * h - o) % 4 for c, h, o in zip(chip, high, offset))
            at = ((x * 4 + z) * 2 + y % 2) * 4 + y // 2 * 2 + core
            base = jnp.where(sublane == j, at * 120, base)
        return (2 * (base + lane8) + 5).astype(F32) * scale

    def widen(group):
        for j in range(GROUP):
            wide[j * WIDE : j * WIDE + 56, :] = spec[group, j][:56].astype(F32)

    def product(q, weight):
        ik, jl, il, jk = (wide[pl.ds(pairs[k, q], GROUP, stride=WIDE), :] for k in range(4))
        prods[pl.ds(q, GROUP, stride=TALL), :] = weight * (ik * jl + il * jk)

    def finish(slot):
        for j in range(GROUP):
            rows = prods[j * TALL : j * TALL + 128, :]
            lhs[slot, :, j * ROWS : (j + 1) * ROWS] = rows.astype(BF16)

    def pattern(slot, group, j, i):
        for h, ref in enumerate((top, low)):
            x = ref[group, j].astype(F32)
            rows = slice(j * ROWS + 64 * h, j * ROWS + 64 * h + 64)
            if i < 8:
                at = half * 64 + (core * 32 + 8 * i) % 64 + lane // 16
                left[slot, i, rows, :] = jnp.take_along_axis(x, at, axis=1).astype(BF16)
            else:
                at = 16 * (i - 8) + lane % 16
                right[slot, i - 8, rows, :] = jnp.take_along_axis(x, at, axis=1).astype(BF16)

    every = [(j, i) for j in range(GROUP) for i in range(16)]

    for p in range(3):
        forward(p, 0, 1)
    widen(0)
    first_weight = weights(0)
    lax.fori_loop(0, 128, lambda q, _: product(q, first_weight), None, unroll=8)
    finish(0)
    for j, i in every:
        pattern(0, 0, j, i)
    for p in range(3):
        forward(p, 3, 1)
        forward(p, 1, 3)
        forward(p, 2, 3)

    def swap(i):
        return pltpu.make_async_remote_copy(
            src_ref=sent.at[i],
            dst_ref=got.at[i],
            send_sem=swap_send.at[i],
            recv_sem=swap_recv.at[i],
            device_id=partner,
            device_id_type=MESH,
        )

    def two(step, _):
        for slot in range(2):
            ahead = step * 2 + slot + 1

            @pl.when(ahead < 8)
            def _():
                arrive(ahead)

            following = ahead % 8
            widen(following)
            weight = weights(following)
            for turn in range(32):
                n = (turn + 16) % 32
                for j, i in every[4 * turn : 4 * turn + 4]:
                    pattern(1 - slot, following, j, i)
                for q in range(4 * turn, 4 * turn + 4):
                    product(q, weight)
                rhs = jnp.concatenate(
                    [left[slot, m // 8] * right[slot, m % 8] for m in (2 * n, 2 * n + 1)], axis=1
                )
                acc[:, n * 256 : (n + 1) * 256] += jnp.dot(
                    lhs[slot], rhs, preferred_element_type=F32
                )
                if slot == 1 and turn == 15:

                    @pl.when(step == 3)
                    def _():
                        for i in range(4):
                            at = 4096 + i * 1024
                            sent[i] = acc[:, at : at + 1024].astype(BF16)
                            swap(i).start()

            finish(1 - slot)

    lax.fori_loop(0, BLOCKS // GROUP // 2, two, None)

    for p in range(3):
        wait(p, parts[p].at[0, pl.ds(0, 3)], send_sem.at[p, 0])
        wait(p, parts[p].at[pl.ds(0, 3), pl.ds(0, 4)], send_sem.at[p, 1])
        wait(p, parts[p].at[pl.ds(0, 6)], send_sem.at[p, 2])
    lane = lax.broadcasted_iota(jnp.int32, (128, 128), 1)
    for i in range(4):
        swap(i).wait()
        v = [
            acc[:, i * 1024 + j * 128 : i * 1024 + (j + 1) * 128]
            + got[i, :, j * 128 : (j + 1) * 128].astype(F32)
            for j in range(8)
        ]
        for k in (1, 2, 4):
            under = (lane // 16) & k == 0
            for m in range(8):
                if m & k == 0:
                    a, b = v[m], v[m + k]
                    v[m] = jnp.where(under, a, pltpu.roll(b, 16 * k, 1))
                    v[m + k] = jnp.where(under, pltpu.roll(a, 128 - 16 * k, 1), b)
        for m in range(8):
            out[i * 8 + m] = v[m]


def covariance(pairs, spectra, kernel, modes):
    vmem = pl.BlockSpec(memory_space=pltpu.VMEM)
    return pl.pallas_call(
        fused,
        out_shape=jax.ShapeDtypeStruct((32, 128, 128), F32),
        in_specs=[pl.BlockSpec(memory_space=pltpu.SMEM), vmem, vmem, vmem],
        out_specs=vmem,
        scratch_shapes=[
            pltpu.VMEM((ROWS + SROWS, 128), BF16),
            pltpu.VMEM((8, 8, 64, 128), BF16),
            pltpu.VMEM((8, 8, 64, 128), BF16),
            pltpu.VMEM((8, 8, 64, 128), BF16),
            pltpu.VMEM((2, 8, GROUP * ROWS, 128), BF16),
            pltpu.VMEM((2, 8, GROUP * ROWS, 128), BF16),
            pltpu.VMEM((2, 128, GROUP * ROWS), BF16),
            pltpu.VMEM((GROUP * WIDE, 128), F32),
            pltpu.VMEM((GROUP * TALL, 128), F32),
            pltpu.VMEM((128, 8192), F32),
            pltpu.VMEM((4, 128, 1024), BF16),
            pltpu.VMEM((4, 128, 1024), BF16),
            pltpu.SemaphoreType.DMA((3,)),
            pltpu.SemaphoreType.DMA((3, 3)),
            pltpu.SemaphoreType.DMA((3, 16)),
            pltpu.SemaphoreType.DMA((4,)),
            pltpu.SemaphoreType.DMA((4,)),
        ],
        compiler_params=pltpu.CompilerParams(
            collective_id=0, has_side_effects=True, vmem_limit_bytes=26 * 2**20
        ),
    )(pairs, spectra, kernel, modes)


def body(spectra, kernel, modes, quads):
    own = lax.dynamic_slice_in_dim(quads, lax.axis_index("tile") * 128, 128, 0).T
    i, j, k, l = own[0], own[1], own[2], own[3]
    pairs = jnp.stack([pair_index(i, k), pair_index(j, l), pair_index(i, l), pair_index(j, k)])
    return covariance(pairs, spectra, kernel, modes)


def solution(mesh):
    return jax.shard_map(
        body,
        mesh=mesh,
        in_specs=(P(None, ("tile", "ell")), P(("tile", "ell"), None), P(), P()),
        out_specs=P("ell", "tile", None),
        check_vma=False,
    )
```

```python
import functools
import math

import jax
import jax.numpy as jnp
from jax import lax
from jax.experimental import pallas as pl
from jax.experimental.pallas import tpu as pltpu
from jax.sharding import PartitionSpec as P

NB = 10
L = 15360
ROWS = 128
SROWS = 64
WIDE = 57
TALL = 129
GROUP = 8
BLOCKS = 64
F32 = jnp.float32
BF16 = jnp.bfloat16
MESH = pl.DeviceIdType.MESH
ORDERS = ((0, 1, 2), (1, 2, 0), (2, 0, 1))


def pair_index(first, second):
    lower = jnp.minimum(first, second)
    upper = jnp.maximum(first, second)
    return lower * NB - lower * (lower - 1) // 2 + upper - lower


def place(e):
    group = e[0] // 2 * 4 + e[1] // 2 * 2 + e[2] // 2
    return group, e[0] % 2 * 4 + e[1] % 2 * 2 + e[2] % 2


def fused(
    pairs, spectra_in, kernel_in, modes_in, out, spectra, kernel, modes, in_sem, local, top, low, spec, left, right, lhs, wide, prods, acc,
    sent, got, own_sem, send_sem, recv_sem, swap_send, swap_recv,
):
    tile, ell = lax.axis_index("tile"), lax.axis_index("ell")
    half, core = ell // 2, ell % 2
    chip = (tile // 8, half * 2 + tile % 2, tile // 2 % 4)
    parts = (top, low, spec)

    def device(x, y, z, on):
        return ((x * 4 + z) * 2 + y % 2, y // 2 * 2 + on)

    def peer(axis, k):
        at = list(chip)
        at[axis] = (at[axis] + k) % 4
        return device(*at, core)

    partner = device(*chip, 1 - core)
    pulls = [
        pltpu.make_async_copy(source, target, in_sem.at[n])
        for n, (source, target) in enumerate(
            ((kernel_in, kernel), (modes_in, modes), (spectra_in, spectra))
        )
    ]
    for pull in pulls:
        pull.start()
    barrier = pltpu.get_barrier_semaphore()
    for axis in range(3):
        for k in (1, 2, 3):
            pl.semaphore_signal(barrier, inc=1, device_id=peer(axis, k), device_id_type=MESH)
    pl.semaphore_signal(barrier, inc=1, device_id=partner, device_id_type=MESH)

    for pull in pulls:
        pull.wait()
    compressed = jnp.dot(kernel[...], modes[...], preferred_element_type=F32)
    local[...] = jnp.zeros_like(local)
    local[:120, :] = compressed.astype(BF16)
    local[128:183, :120] = spectra[...].astype(BF16)
    acc[...] = jnp.zeros_like(acc)
    pl.semaphore_wait(barrier, 10)

    def send(p, src, dst, axis, k, send_at, recv_at):
        pltpu.make_async_remote_copy(
            src_ref=src,
            dst_ref=parts[p].at[place(dst)],
            send_sem=send_sem.at[p, send_at],
            recv_sem=recv_sem.at[p, recv_at],
            device_id=peer(axis, k),
            device_id_type=MESH,
        ).start()

    def wait(p, ref, sem):
        pltpu.make_async_copy(ref, ref, sem).wait()

    for p, (d1, d2, d3) in enumerate(ORDERS):
        mine = local.at[pl.ds(64 * p, 64)]
        pltpu.make_async_copy(mine, parts[p].at[0, 0], own_sem.at[p]).start()
        for k in (1, 2, 3):
            e = [0, 0, 0]
            e[d1] = k
            send(p, mine, e, d1, k, 0, 0)
    for p, (d1, d2, d3) in enumerate(ORDERS):
        wait(p, parts[p].at[0, 0], own_sem.at[p])
        wait(p, parts[p].at[0, pl.ds(0, 3)], recv_sem.at[p, 0])
        for step in range(4):
            for k, m in ((1, step), (3, 3 - step)):
                e = [0, 0, 0]
                e[d1] = m
                src = parts[p].at[place(e)]
                e[d2] = k
                on = {(1, True): 1, (3, False): 2}.get((k, m < 2), 3)
                send(p, src, e, d2, k, 1, on)
    for p, (d1, d2, d3) in enumerate(ORDERS):
        for k, lines in ((1, (0, 1)), (3, (2, 3))):
            wait(p, parts[p].at[0, pl.ds(0, 2)], recv_sem.at[p, 1 + k // 2])
            for m in lines:
                e = [0, 0, 0]
                e[d1], e[d2] = m, k
                src = parts[p].at[place(e)]
                e[d2] = 2
                send(p, src, e, d2, k, 1, 3)

    def four(p, quarter, came, k, lands):
        d1, d2, d3 = ORDERS[p]
        for m in range(4):
            e = [0, 0, 0]
            e[d1], e[d2], e[d3] = quarter // 2 * 2 + m // 2, quarter % 2 * 2 + m % 2, came
            src = parts[p].at[place(e)]
            e[d3] = lands
            send(p, src, e, d3, k, 2, 4 + 3 * quarter + lands - 1)

    def landed(p, quarter, k):
        wait(p, parts[p].at[0, pl.ds(0, 4)], recv_sem.at[p, 4 + 3 * quarter + k - 1])

    def forward(p, quarter, k):
        landed(p, quarter, k)
        four(p, quarter, k, k, 2)

    for p in range(3):
        wait(p, parts[p].at[0], recv_sem.at[p, 3])
        for ahead, back in ((0, 1), (3, 2)):
            four(p, ahead, 0, 1, 1)
            four(p, back, 0, 3, 3)
    for p in range(3):
        for ahead, back in ((1, 0), (2, 3)):
            four(p, ahead, 0, 1, 1)
            four(p, back, 0, 3, 3)

    def arrive(group):
        high = (group // 4, group // 2 % 2, group % 2)
        for p, (d1, d2, d3) in enumerate(ORDERS):
            quarter = 2 * high[d1] + high[d2]
            mixed = (high[d1] + high[d2]) % 2

            @pl.when((1 - high[d3]) * mixed == 1)
            def _():
                landed(p, quarter, 1)

            @pl.when(high[d3] == 1)
            def _():
                landed(p, quarter, 2)

            @pl.when(high[d3] * (1 - mixed) == 1)
            def _():
                landed(p, quarter, 3)

    lane = lax.broadcasted_iota(jnp.int32, (64, 128), 1)
    sublane = lax.broadcasted_iota(jnp.int32, (GROUP, 128), 0)
    lane8 = lax.broadcasted_iota(jnp.int32, (GROUP, 128), 1)
    scale = 0.5 / math.sqrt(L)

    def weights(group):
        base = jnp.zeros((GROUP, 128), jnp.int32)
        high = (group // 4, group // 2 % 2, group % 2)
        for j in range(GROUP):
            offset = (j // 4, j // 2 % 2, j % 2)
            x, y, z = ((c + 4 - 2 * h - o) % 4 for c, h, o in zip(chip, high, offset))
            at = ((x * 4 + z) * 2 + y % 2) * 4 + y // 2 * 2 + core
            base = jnp.where(sublane == j, at * 120, base)
        return (2 * (base + lane8) + 5).astype(F32) * scale

    def widen(group):
        for j in range(GROUP):
            wide[j * WIDE : j * WIDE + 56, :] = spec[group, j][:56].astype(F32)

    def product(q, weight):
        ik, jl, il, jk = (wide[pl.ds(pairs[k, q], GROUP, stride=WIDE), :] for k in range(4))
        prods[pl.ds(q, GROUP, stride=TALL), :] = weight * (ik * jl + il * jk)

    def finish(slot):
        for j in range(GROUP):
            rows = prods[j * TALL : j * TALL + 128, :]
            lhs[slot, :, j * ROWS : (j + 1) * ROWS] = rows.astype(BF16)

    def pattern(slot, group, j, i):
        for h, ref in enumerate((top, low)):
            x = ref[group, j].astype(F32)
            rows = slice(j * ROWS + 64 * h, j * ROWS + 64 * h + 64)
            if i < 8:
                at = half * 64 + (core * 32 + 8 * i) % 64 + lane // 16
                left[slot, i, rows, :] = jnp.take_along_axis(x, at, axis=1).astype(BF16)
            else:
                at = 16 * (i - 8) + lane % 16
                right[slot, i - 8, rows, :] = jnp.take_along_axis(x, at, axis=1).astype(BF16)

    every = [(j, i) for j in range(GROUP) for i in range(16)]

    for p in range(3):
        forward(p, 0, 1)
    widen(0)
    first_weight = weights(0)
    lax.fori_loop(0, 128, lambda q, _: product(q, first_weight), None, unroll=8)
    finish(0)
    for j, i in every:
        pattern(0, 0, j, i)
    for p in range(3):
        forward(p, 3, 1)
        forward(p, 1, 3)
        forward(p, 2, 3)

    def swap(i):
        return pltpu.make_async_remote_copy(
            src_ref=sent.at[i],
            dst_ref=got.at[i],
            send_sem=swap_send.at[i],
            recv_sem=swap_recv.at[i],
            device_id=partner,
            device_id_type=MESH,
        )

    def two(step, _):
        for slot in range(2):
            ahead = step * 2 + slot + 1

            @pl.when(ahead < 8)
            def _():
                arrive(ahead)

            following = ahead % 8
            widen(following)
            weight = weights(following)
            for turn in range(32):
                n = (turn + 16) % 32
                for j, i in every[4 * turn : 4 * turn + 4]:
                    pattern(1 - slot, following, j, i)
                for q in range(4 * turn, 4 * turn + 4):
                    product(q, weight)
                rhs = jnp.concatenate(
                    [left[slot, m // 8] * right[slot, m % 8] for m in (2 * n, 2 * n + 1)], axis=1
                )
                acc[:, n * 256 : (n + 1) * 256] += jnp.dot(
                    lhs[slot], rhs, preferred_element_type=F32
                )
                if slot == 1 and turn == 15:

                    @pl.when(step == 3)
                    def _():
                        for i in range(4):
                            at = 4096 + i * 1024
                            sent[i] = acc[:, at : at + 1024].astype(BF16)
                            swap(i).start()

            finish(1 - slot)

    lax.fori_loop(0, BLOCKS // GROUP // 2, two, None)

    for p in range(3):
        wait(p, parts[p].at[0, pl.ds(0, 3)], send_sem.at[p, 0])
        wait(p, parts[p].at[pl.ds(0, 3), pl.ds(0, 4)], send_sem.at[p, 1])
        wait(p, parts[p].at[pl.ds(0, 6)], send_sem.at[p, 2])
    lane = lax.broadcasted_iota(jnp.int32, (128, 128), 1)
    for i in range(4):
        swap(i).wait()
        v = [
            acc[:, i * 1024 + j * 128 : i * 1024 + (j + 1) * 128]
            + got[i, :, j * 128 : (j + 1) * 128].astype(F32)
            for j in range(8)
        ]
        for k in (1, 2, 4):
            under = (lane // 16) & k == 0
            for m in range(8):
                if m & k == 0:
                    a, b = v[m], v[m + k]
                    v[m] = jnp.where(under, a, pltpu.roll(b, 16 * k, 1))
                    v[m + k] = jnp.where(under, pltpu.roll(a, 128 - 16 * k, 1), b)
        for m in range(8):
            out[i * 8 + m] = v[m]


def covariance(pairs, spectra, kernel, modes):
    vmem = pl.BlockSpec(memory_space=pltpu.VMEM)
    return pl.pallas_call(
        fused,
        out_shape=jax.ShapeDtypeStruct((32, 128, 128), F32),
        in_specs=[pl.BlockSpec(memory_space=pltpu.SMEM)]
        + [pl.BlockSpec(memory_space=pltpu.HBM)] * 3,
        out_specs=vmem,
        scratch_shapes=[
            pltpu.VMEM(spectra.shape, F32),
            pltpu.VMEM(kernel.shape, BF16),
            pltpu.VMEM(modes.shape, BF16),
            pltpu.SemaphoreType.DMA((3,)),
            pltpu.VMEM((ROWS + SROWS, 128), BF16),
            pltpu.VMEM((8, 8, 64, 128), BF16),
            pltpu.VMEM((8, 8, 64, 128), BF16),
            pltpu.VMEM((8, 8, 64, 128), BF16),
            pltpu.VMEM((2, 8, GROUP * ROWS, 128), BF16),
            pltpu.VMEM((2, 8, GROUP * ROWS, 128), BF16),
            pltpu.VMEM((2, 128, GROUP * ROWS), BF16),
            pltpu.VMEM((GROUP * WIDE, 128), F32),
            pltpu.VMEM((GROUP * TALL, 128), F32),
            pltpu.VMEM((128, 8192), F32),
            pltpu.VMEM((4, 128, 1024), BF16),
            pltpu.VMEM((4, 128, 1024), BF16),
            pltpu.SemaphoreType.DMA((3,)),
            pltpu.SemaphoreType.DMA((3, 3)),
            pltpu.SemaphoreType.DMA((3, 16)),
            pltpu.SemaphoreType.DMA((4,)),
            pltpu.SemaphoreType.DMA((4,)),
        ],
        compiler_params=pltpu.CompilerParams(
            collective_id=0, has_side_effects=True, vmem_limit_bytes=26 * 2**20
        ),
    )(pairs, *(pltpu.with_memory_space_constraint(a, pltpu.HBM) for a in (spectra, kernel, modes)))


def body(spectra, kernel, modes, quads):
    own = lax.dynamic_slice_in_dim(quads, lax.axis_index("tile") * 128, 128, 0).T
    i, j, k, l = own[0], own[1], own[2], own[3]
    pairs = jnp.stack([pair_index(i, k), pair_index(j, l), pair_index(i, l), pair_index(j, k)])
    return covariance(pairs, spectra, kernel, modes)


def solution(mesh):
    return jax.shard_map(
        body,
        mesh=mesh,
        in_specs=(P(None, ("tile", "ell")), P(("tile", "ell"), None), P(), P()),
        out_specs=P("ell", "tile", None),
        check_vma=False,
    )
```
